256 devices in a mesh: depth: 8 (over y, core), lat: 32 (over z, x).
Axes of the slice: x: 4, y: 4, z: 8, core: 2. Of those that a mesh axis runs over, the one named last changes fastest.
Arguments:
- leaf_blocks: float32 [8, 16384, 512], P('depth', 'lat'), may hold values from -0.25 to 0.25
- mix_left: float32 [8, 5, 16384, 256], P('depth', None, 'lat'), may hold values from -0.375 to 0.375
- mix_right: float32 [8, 5, 16384, 256], P('depth', None, 'lat'), may hold values from -0.25 to 0.25
- source_cells: int32 [8, 768], P('depth'), may hold values from 0 to 16383
- source_amps: float32 [8, 768], P('depth'), may hold values from -6 to 6
- plan: int32 [768], replicated, may hold values from 0 to 767, each once
Outputs:
- traces: float32 [8, 6, 16384, 128], P('depth', None, 'lat')
The draws below stay inside these ranges and needn't reach their ends.
Inputs may be any that keep to these rules, and one draw needn't show every extreme that they name: `plan`: every shot appears exactly once.
All inputs are finite; a program needn't handle non-finite values.
Results may differ from the reference program's by a relative error of at most 0.00017.
Values sent between devices are 32-bit elements; how exact they have to be, the bound alone decides.
No kernel may reach another device: no remote copies, remote signals or barrier semaphores. Data moves between devices by JAX's collectives and lax.ppermute only.
A program may use at most 64 MiB of HBM per device.

```python
import math
import jax
import jax.numpy as jnp
from jax import lax

N = 16384
RANK = 256
COLS = 128
FRONTS = 6
LAYERS = 8
BLOCKS = 32
ROWS = 512
LEVELS = 5
SHOTS = 768


def plant(values, own_key, smallest, high):
    extent = values.shape
    spot = [jax.random.randint(jax.random.fold_in(own_key, axis), (), 0, extent[axis]) for axis in range(len(extent))]
    values = values.at[tuple(spot)].set(smallest)
    longest = extent.index(max(extent))
    spot[longest] = (spot[longest] + 1) % extent[longest]
    return values.at[tuple(spot)].set(high)


def block_scale(own_key, shape, cuts, low, high):
    level = 1.0
    for axis_at, shards_of in cuts:
        heights = jax.random.uniform(jax.random.fold_in(jax.random.fold_in(own_key, 6), axis_at), (shards_of,), jnp.float32, low / len(cuts), high / len(cuts))
        level = level * jnp.repeat(jnp.exp(heights), shape[axis_at] // shards_of).reshape((-1,) + (1,) * (len(shape) - 1 - axis_at))
    return level


def scatter_about(rng, extent, width, bound, cuts=(), kind=jnp.bfloat16):
    factor_of = block_scale(rng, extent, cuts, -0.22, 0.18) if cuts else 1.0
    entries = jax.random.normal(rng, extent, jnp.float32) * width * factor_of
    return jnp.minimum(jnp.maximum(entries, -bound), bound).astype(kind)


def setup_inputs(seed: int = 0) -> dict:
    key_list = jax.random.split(jax.random.key(seed), 7)
    return {
        "leaf_blocks": scatter_about(key_list[0], (LAYERS, N, ROWS), ROWS ** -0.5, 0.25, ((0, 8), (1, 32)), jnp.float32),
        "mix_left": scatter_about(key_list[1], (LAYERS, LEVELS, N, RANK), RANK ** -0.5, 0.375, ((0, 8), (2, 32)), jnp.float32),
        "mix_right": scatter_about(key_list[2], (LAYERS, LEVELS, N, RANK), ROWS ** -0.5, 0.25, ((0, 8), (2, 32)), jnp.float32),
        "source_cells": plant(jax.random.randint(key_list[3], (LAYERS, SHOTS), 0, N), jax.random.fold_in(key_list[3], 1), 0, N - 1).astype(jnp.int32),
        "source_amps": scatter_about(key_list[4], (LAYERS, SHOTS), 1.0, 6.0, ((0, 8),), jnp.float32),
        "plan": jax.random.permutation(key_list[5], SHOTS).astype(jnp.int32),
    }


def reference(leaf_blocks, mix_left, mix_right, source_cells, source_amps, plan):
    highest = lax.Precision.HIGHEST
    halving = 1.0 / math.sqrt(2.0)
    block_ids = jnp.arange(BLOCKS, dtype=jnp.int32)
    cell_ids = jnp.arange(N, dtype=jnp.int32)
    trace = jnp.zeros((N, SHOTS), jnp.float32)
    outputs = []
    for layer_index in range(LAYERS):
        cell_order = source_cells[layer_index][plan]
        amp_order = source_amps[layer_index][plan] * math.sqrt(N)
        source = jnp.where(cell_ids[:, None] == cell_order[None, :], amp_order[None, :], 0.0)
        inputs = (trace + source).reshape(BLOCKS, ROWS, SHOTS)
        leaf = leaf_blocks[layer_index].reshape(BLOCKS, ROWS, ROWS)
        mixed = jnp.einsum('brs,bsc->brc', leaf, inputs, precision=highest)
        for level_bit in range(LEVELS):
            right = mix_right[layer_index, level_bit].reshape(BLOCKS, ROWS, RANK)
            left = mix_left[layer_index, level_bit].reshape(BLOCKS, ROWS, RANK)
            compressed = jnp.einsum('brk,brc->bkc', right, mixed, precision=highest)
            partner = compressed[jnp.bitwise_xor(block_ids, 1 << level_bit)]
            mixed = (mixed + jnp.einsum('brk,bkc->brc', left, partner, precision=highest)) * halving
        trace = mixed.reshape(N, SHOTS)
        outputs.append(trace.reshape(N, FRONTS, COLS).transpose(1, 0, 2))
    return jnp.stack(outputs)
```

```python
import functools
import math

import jax
import jax.numpy as jnp
from jax import lax
from jax.experimental import pallas as pl
from jax.experimental.pallas import tpu as pltpu
from jax.sharding import PartitionSpec as P

N = 16384
FRONTS = 6
STREAMS = 2
GROUPS = 2
HALVING = 1.0 / math.sqrt(2.0)
NT = (((1,), (1,)), ((), ()))
NN = (((1,), (0,)), ((), ()))


def lat_swap(x, bit):
    count = lax.axis_size("lat")
    return lax.ppermute(x, "lat", [(i, i ^ bit) for i in range(count)])


def core_swap(x):
    count = lax.axis_size("depth")
    return lax.ppermute(x, "depth", [(i, i ^ 1) for i in range(count)])


def next_stage(x):
    count = lax.axis_size("depth")
    return lax.ppermute(x, "depth", [(i, i + 2) for i in range(count - 2)])


def split(x):
    high = x.astype(jnp.bfloat16)
    low = (x - high.astype(jnp.float32)).astype(jnp.bfloat16)
    return high, low


def mm(x, w_high, w_low, dims):
    rows = x.shape[0]
    high, low = split(x)
    both = jnp.concatenate([high, low], axis=0)
    main = lax.dot_general(both, w_high, dims, preferred_element_type=jnp.float32)
    rest = lax.dot_general(high, w_low, dims, preferred_element_type=jnp.float32)
    return main[:rows] + (main[rows:] + rest)


def begin_layer(v, source_ref, layer, lh, ll, rh, rl, y_ref, c_ref, z_ref):
    cells = source_ref[:, 2 * layer : 2 * layer + 1]
    amps = source_ref[:, 2 * layer + 1 : 2 * layer + 2]
    rows = lax.broadcasted_iota(jnp.int32, v.shape, 1).astype(jnp.float32)
    v = v + jnp.where(rows == cells, amps, 0.0)
    y = mm(v, lh[layer], ll[layer], NT)
    y_ref[...] = y
    c_ref[...] = mm(y, rh[layer, 0], rl[layer, 0], NN)
    z_ref[...] = mm(y, rh[layer, 1], rl[layer, 1], NN)


def pair_step(y, a, b, e, layer, level, kh, kl, mh, ml):
    link = 0 if level == 0 else 1
    inner = HALVING * (e + mm(b, kh[layer, link], kl[layer, link], NN))
    y = HALVING * (y + mm(a, mh[layer, level], ml[layer, level], NT))
    return HALVING * (y + mm(inner, mh[layer, level + 1], ml[layer, level + 1], NT))


def kernel_1(layer, v, source, lh, ll, rh, rl, y_ref, c_ref, z_ref):
    begin_layer(v[...], source, layer, lh, ll, rh, rl, y_ref, c_ref, z_ref)


def kernel_2(layer, y, a, b, e, kh, kl, mh, ml, rh, rl, y_ref, c_ref):
    out = pair_step(y[...], a[...], b[...], e[...], layer, 0, kh, kl, mh, ml)
    y_ref[...] = out
    c_ref[...] = mm(out, rh[layer, 2], rl[layer, 2], NN)


def kernel_3(layer, y, a, mh, ml, rh, rl, y_ref, c_ref, z_ref):
    out = HALVING * (y[...] + mm(a[...], mh[layer, 2], ml[layer, 2], NT))
    y_ref[...] = out
    c_ref[...] = mm(out, rh[layer, 3], rl[layer, 3], NN)
    z_ref[...] = mm(out, rh[layer, 4], rl[layer, 4], NN)


def kernel_4(layer, place, y, a, b, e, kh, kl, mh, ml, kept_in, t_ref, kept, sem):
    t_ref[...] = pair_step(y[...], a[...], b[...], e[...], layer, 3, kh, kl, mh, ml)
    copy = pltpu.make_async_copy(t_ref, kept.at[place], sem)
    copy.start()
    copy.wait()


def kernel_41(layer, place, y, a, b, e, source, kh, kl, mh, ml, lh, ll, rh, rl, kept_in, y_ref, c_ref, z_ref, kept, t, sem):
    out = pair_step(y[...], a[...], b[...], e[...], layer, 3, kh, kl, mh, ml)
    t[...] = out
    copy = pltpu.make_async_copy(t, kept.at[place], sem)
    copy.start()
    begin_layer(out, source, layer + 1, lh, ll, rh, rl, y_ref, c_ref, z_ref)
    copy.wait()


def kernel_split(own, count, core, *refs):
    sources, outs = refs[:count], refs[-2 * count :]
    slot = core[0] if own else 1 - core[0]
    for n in range(count):
        high, low = split(sources[n][...])
        outs[2 * n][slot] = high
        outs[2 * n + 1][slot] = low


IN_VMEM = pl.BlockSpec(memory_space=pltpu.VMEM)
IN_SMEM = pl.BlockSpec(memory_space=pltpu.SMEM)
IN_HBM = pl.BlockSpec(memory_space=pl.ANY)
PARAMS = pltpu.CompilerParams(vmem_limit_bytes=20 << 20)


def held(x):
    return pltpu.with_memory_space_constraint(x, pltpu.VMEM) if x.dtype == jnp.bfloat16 else x


def run(kernel, arrays, widths, kept=None, scratch=()):
    rows = arrays[0].shape[0]
    shapes = [jax.ShapeDtypeStruct((rows, width), jnp.float32) for width in widths]
    in_specs = [IN_VMEM] * len(arrays)
    out_specs = [IN_VMEM] * len(widths)
    operands = [held(x) for x in arrays]
    aliases = {}
    if kept is not None:
        aliases = {len(operands): len(shapes)}
        operands.append(pltpu.with_memory_space_constraint(kept, pltpu.HBM))
        in_specs.append(IN_HBM)
        out_specs.append(IN_HBM)
        shapes.append(jax.ShapeDtypeStruct(kept.shape, kept.dtype))
    return pl.pallas_call(
        kernel,
        out_shape=shapes,
        in_specs=in_specs,
        out_specs=out_specs,
        scratch_shapes=scratch,
        input_output_aliases=aliases,
        compiler_params=PARAMS,
    )(*operands)


def split_into(core, arrays, filled=None):
    count = len(arrays)
    shapes = [jax.ShapeDtypeStruct((2, *x.shape), jnp.bfloat16) for x in arrays for _ in range(2)]
    operands = [core] + list(arrays) + [held(x) for x in filled or []]
    return pl.pallas_call(
        functools.partial(kernel_split, filled is None, count),
        out_shape=shapes,
        in_specs=[IN_SMEM] + [IN_VMEM] * (len(operands) - 1),
        out_specs=[IN_VMEM] * len(shapes),
        input_output_aliases={1 + count + n: n for n in range(len(filled or []))},
        compiler_params=pltpu.CompilerParams(vmem_limit_bytes=24 << 20),
    )(*operands)


def on_device(leaf_blocks, mix_left, mix_right, source_cells, source_amps, plan):
    depth_index = lax.axis_index("depth")
    core = lax.rem(depth_index, 2)
    stage = depth_index // 2
    stages = lax.axis_size("depth") // 2
    row_count = leaf_blocks.shape[1]
    rank = mix_left.shape[3]
    shots = plan.shape[0]
    front_cols = shots // FRONTS
    own_cols = shots // 2
    group_cols = own_cols // GROUPS
    piece = group_cols // STREAMS
    ticks = GROUPS + stages - 1

    table = jnp.concatenate([source_cells.astype(jnp.float32), source_amps * math.sqrt(N)], axis=0)
    swapped = core_swap(table)
    table = jnp.concatenate(
        [jnp.where(core == 0, table, swapped), jnp.where(core == 0, swapped, table)], axis=0
    )
    weights = [leaf_blocks[0], mix_right[0], mix_left[0]]
    others = [core_swap(x) for x in weights]

    def joined(level):
        return lax.dot_general(
            mix_left[0, level],
            mix_right[0, level + 1],
            (((0,), (0,)), ((), ())),
            precision=lax.Precision.HIGHEST,
            preferred_element_type=jnp.float32,
        )

    links = jnp.stack([lat_swap(joined(0), 2), lat_swap(joined(3), 16)])
    slot = core[None]
    lh, ll, rh, rl, mh, ml = split_into(slot, others, split_into(slot, weights))
    kh, kl = split_into(slot, [core_swap(links)], split_into(slot, [links]))

    order = lax.dynamic_slice_in_dim(plan, core * own_cols, own_cols)
    chosen = (order[:, None] == jnp.arange(shots, dtype=plan.dtype)[None, :]).astype(jnp.float32)
    base = (lax.axis_index("lat") * row_count).astype(jnp.float32)
    shift = jnp.stack([base, jnp.zeros_like(base), base, jnp.zeros_like(base)])
    sources = (
        lax.dot_general(
            chosen,
            table,
            NT,
            precision=lax.Precision.HIGHEST,
            preferred_element_type=jnp.float32,
        )
        - shift[None, :]
    )

    wide, narrow = row_count, rank

    def outer_round(c, z, near, far):
        return lat_swap(z, far), lat_swap(c, near), lat_swap(c, near | far)

    which = range(STREAMS)
    kept = jnp.zeros((ticks, 2, STREAMS, piece, row_count), jnp.float32)
    carried = [jnp.zeros((piece, row_count), jnp.float32) for _ in which]
    for tick in range(ticks):
        group = jnp.clip(tick - stage, 0, GROUPS - 1)
        parts = [
            lax.dynamic_slice_in_dim(sources, group * group_cols + s * piece, piece) for s in which
        ]
        state = [
            run(
                functools.partial(kernel_1, 0),
                [carried[s], parts[s], lh, ll, rh, rl],
                (wide, narrow, narrow),
            )
            for s in which
        ]
        for layer in range(2):
            got = [outer_round(state[s][1], state[s][2], 1, 2) for s in which]
            state = [
                run(
                    functools.partial(kernel_2, layer),
                    [state[s][0], got[s][1], got[s][2], got[s][0], kh, kl, mh, ml, rh, rl],
                    (wide, narrow),
                )
                for s in which
            ]
            mid = [lat_swap(state[s][1], 4) for s in which]
            state = [
                run(
                    functools.partial(kernel_3, layer),
                    [state[s][0], mid[s], mh, ml, rh, rl],
                    (wide, narrow, narrow),
                )
                for s in which
            ]
            got = [outer_round(state[s][1], state[s][2], 8, 16) for s in which]
            following = []
            for s in which:
                inputs = [state[s][0], got[s][1], got[s][2], got[s][0]]
                if layer == 0:
                    *rest, kept = run(
                        functools.partial(kernel_41, layer, (tick, layer, s)),
                        [*inputs, parts[s], kh, kl, mh, ml, lh, ll, rh, rl],
                        (wide, narrow, narrow),
                        kept,
                        [pltpu.VMEM((piece, row_count), jnp.float32), pltpu.SemaphoreType.DMA],
                    )
                    following.append(rest)
                else:
                    trace, kept = run(
                        functools.partial(kernel_4, layer, (tick, layer, s)),
                        [*inputs, kh, kl, mh, ml],
                        (wide,),
                        kept,
                        [pltpu.SemaphoreType.DMA],
                    )
                    if tick < ticks - 1:
                        following.append(next_stage(trace))
            state = following
        carried = state

    def taken(layer):
        zero = jnp.zeros_like(stage)
        rows = lax.dynamic_slice(
            kept, (stage, layer, zero, zero, zero), (GROUPS, 1, STREAMS, piece, row_count)
        )
        return rows.reshape(FRONTS // 2, front_cols, row_count)

    own, other = taken(core), core_swap(taken(1 - core))
    fronts = jnp.concatenate([jnp.where(core == 0, own, other), jnp.where(core == 0, other, own)])
    return fronts.transpose(0, 2, 1)[None]


def solution(mesh):
    return jax.shard_map(
        on_device,
        mesh=mesh,
        in_specs=(
            P("depth", "lat", None),
            P("depth", None, "lat", None),
            P("depth", None, "lat", None),
            P("depth", None),
            P("depth", None),
            P(),
        ),
        out_specs=P("depth", None, "lat", None),
        check_vma=False,
    )
```

```python
import functools
import math

import jax
import jax.numpy as jnp
from jax import lax
from jax.experimental import pallas as pl
from jax.experimental.pallas import tpu as pltpu
from jax.sharding import PartitionSpec as P


N = 16384
FRONTS = 6
STREAMS = 2
GROUPS = 2
HALVING = 1.0 / math.sqrt(2.0)
NT = (((1,), (1,)), ((), ()))
NN = (((1,), (0,)), ((), ()))


def lat_swap(x, bit):
    count = lax.axis_size("lat")
    return lax.ppermute(x, "lat", [(i, i ^ bit) for i in range(count)])


def core_swap(x):
    count = lax.axis_size("depth")
    return lax.ppermute(x, "depth", [(i, i ^ 1) for i in range(count)])


def next_stage(x):
    count = lax.axis_size("depth")
    return lax.ppermute(x, "depth", [(i, i + 2) for i in range(count - 2)])


def split(x):
    high = x.astype(jnp.bfloat16)
    low = (x - high.astype(jnp.float32)).astype(jnp.bfloat16)
    return high, low


def mm(x, w_high, w_low, dims):
    rows = x.shape[0]
    high, low = split(x)
    both = jnp.concatenate([high, low], axis=0)
    main = lax.dot_general(both, w_high, dims, preferred_element_type=jnp.float32)
    rest = lax.dot_general(high, w_low, dims, preferred_element_type=jnp.float32)
    return main[:rows] + (main[rows:] + rest)


def begin_layer(v, source_ref, layer, lh, ll, rh, rl, y_ref, c_ref, z_ref):
    cells = source_ref[:, 2 * layer : 2 * layer + 1]
    amps = source_ref[:, 2 * layer + 1 : 2 * layer + 2]
    rows = lax.broadcasted_iota(jnp.int32, v.shape, 1).astype(jnp.float32)
    v = v + jnp.where(rows == cells, amps, 0.0)
    y = mm(v, lh[layer, 0], ll[layer, 0], NT)
    y_ref[...] = y
    c_ref[...] = mm(y, rh[layer, 0], rl[layer, 0], NN)
    z_ref[...] = mm(y, rh[layer, 1], rl[layer, 1], NN)


def pair_step(y, a, b, e, layer, level, kh, kl, mh, ml):
    link = 0 if level == 0 else 1
    inner = HALVING * (e + mm(b, kh[layer, link], kl[layer, link], NN))
    y = HALVING * (y + mm(a, mh[layer, level], ml[layer, level], NT))
    return HALVING * (y + mm(inner, mh[layer, level + 1], ml[layer, level + 1], NT))


def kernel_1(layer, v, source, lh, ll, rh, rl, y_ref, c_ref, z_ref):
    begin_layer(v[...], source, layer, lh, ll, rh, rl, y_ref, c_ref, z_ref)


def kernel_2(layer, y, a, b, e, kh, kl, mh, ml, rh, rl, y_ref, c_ref):
    out = pair_step(y[...], a[...], b[...], e[...], layer, 0, kh, kl, mh, ml)
    y_ref[...] = out
    c_ref[...] = mm(out, rh[layer, 2], rl[layer, 2], NN)


def kernel_3(layer, y, a, mh, ml, rh, rl, y_ref, c_ref, z_ref):
    out = HALVING * (y[...] + mm(a[...], mh[layer, 2], ml[layer, 2], NT))
    y_ref[...] = out
    c_ref[...] = mm(out, rh[layer, 3], rl[layer, 3], NN)
    z_ref[...] = mm(out, rh[layer, 4], rl[layer, 4], NN)


def kernel_4(layer, place, y, a, b, e, kh, kl, mh, ml, kept_in, t_ref, kept, sem):
    t_ref[...] = pair_step(y[...], a[...], b[...], e[...], layer, 3, kh, kl, mh, ml)
    copy = pltpu.make_async_copy(t_ref, kept.at[place], sem)
    copy.start()
    copy.wait()


def kernel_41(layer, place, y, a, b, e, source, kh, kl, mh, ml, lh, ll, rh, rl, kept_in, y_ref, c_ref, z_ref, kept, t, sem):
    out = pair_step(y[...], a[...], b[...], e[...], layer, 3, kh, kl, mh, ml)
    t[...] = out
    copy = pltpu.make_async_copy(t, kept.at[place], sem)
    copy.start()
    begin_layer(out, source, layer + 1, lh, ll, rh, rl, y_ref, c_ref, z_ref)
    copy.wait()


def kernel_split(count, fills, slots, *refs):
    groups = [refs[count * n : count * (n + 1)] for n in range(fills)]
    outs = refs[-(3 * count + 1) : -(count + 1)]
    buffers, sems = refs[-(count + 1) : -1], refs[-1]
    for n, sources in enumerate(groups):
        copies = []
        for m in range(count):
            for level in range(buffers[m].shape[0]):
                sem = sems.at[len(copies)]
                copies.append((m, level, pltpu.make_async_copy(sources[m].at[level], buffers[m].at[level], sem)))
        for _, _, copy in copies:
            copy.start()
        for m, level, copy in copies:
            copy.wait()
            high, low = split(buffers[m][level])
            outs[2 * m][slots[n], level] = high
            outs[2 * m + 1][slots[n], level] = low


def kernel_after(*refs):
    del refs


IN_VMEM = pl.BlockSpec(memory_space=pltpu.VMEM)
IN_SMEM = pl.BlockSpec(memory_space=pltpu.SMEM)
IN_HBM = pl.BlockSpec(memory_space=pl.ANY)
PARAMS = pltpu.CompilerParams(vmem_limit_bytes=6 << 20)


def held(x):
    return pltpu.with_memory_space_constraint(x, pltpu.VMEM) if x.dtype == jnp.bfloat16 else x


def run(kernel, arrays, widths, kept=None, scratch=()):
    rows = arrays[0].shape[0]
    shapes = [jax.ShapeDtypeStruct((rows, width), jnp.float32) for width in widths]
    in_specs = [IN_VMEM] * len(arrays)
    out_specs = [IN_VMEM] * len(widths)
    operands = [held(x) for x in arrays]
    aliases = {}
    if kept is not None:
        aliases = {len(operands): len(shapes)}
        operands.append(pltpu.with_memory_space_constraint(kept, pltpu.HBM))
        in_specs.append(IN_HBM)
        out_specs.append(IN_HBM)
        shapes.append(jax.ShapeDtypeStruct(kept.shape, kept.dtype))
    return pl.pallas_call(
        kernel,
        out_shape=shapes,
        in_specs=in_specs,
        out_specs=out_specs,
        scratch_shapes=scratch,
        input_output_aliases=aliases,
        compiler_params=PARAMS,
    )(*operands)


def split_into(slots, total, groups, filled=None):
    count = len(groups[0])
    shapes = [
        pltpu.VMEM((total, *x.shape), jnp.bfloat16) for x in groups[0] for _ in range(2)
    ]
    sources = [pltpu.with_memory_space_constraint(x, pltpu.HBM) for group in groups for x in group]
    earlier = [held(x) for x in filled or []]
    chunks = sum(x.shape[0] for x in groups[0])
    return pl.pallas_call(
        functools.partial(kernel_split, count, len(groups)),
        out_shape=shapes,
        in_specs=[IN_SMEM] + [IN_HBM] * len(sources) + [IN_VMEM] * len(earlier),
        out_specs=[IN_VMEM] * len(shapes),
        scratch_shapes=[pltpu.VMEM(x.shape, jnp.float32) for x in groups[0]]
        + [pltpu.SemaphoreType.DMA((chunks,))],
        input_output_aliases={1 + len(sources) + n: n for n in range(len(earlier))},
        compiler_params=pltpu.CompilerParams(vmem_limit_bytes=10 << 20),
    )(jnp.stack(slots), *sources, *earlier)


def after(arrays, value):
    operands = [pltpu.with_memory_space_constraint(x, pltpu.HBM) for x in arrays]
    return pl.pallas_call(
        kernel_after,
        out_shape=[jax.ShapeDtypeStruct(x.shape, x.dtype) for x in arrays],
        in_specs=[IN_HBM] * (len(arrays) + 1),
        out_specs=[IN_HBM] * len(arrays),
        input_output_aliases={n: n for n in range(len(arrays))},
        compiler_params=pltpu.CompilerParams(vmem_limit_bytes=1 << 20),
    )(*operands, value)


def on_device(leaf_blocks, mix_left, mix_right, source_cells, source_amps, plan):
    depth_index = lax.axis_index("depth")
    core = lax.rem(depth_index, 2)
    stage = depth_index // 2
    stages = lax.axis_size("depth") // 2
    row_count = leaf_blocks.shape[1]
    rank = mix_left.shape[3]
    shots = plan.shape[0]
    front_cols = shots // FRONTS
    own_cols = shots // 2
    group_cols = own_cols // GROUPS
    piece = group_cols // STREAMS
    ticks = GROUPS + stages - 1

    table = jnp.concatenate([source_cells.astype(jnp.float32), source_amps * math.sqrt(N)], axis=0)
    swapped = core_swap(table)
    table = jnp.concatenate(
        [jnp.where(core == 0, table, swapped), jnp.where(core == 0, swapped, table)], axis=0
    )
    weights = [leaf_blocks, mix_right[0], mix_left[0]]
    others = [core_swap(x) for x in weights]

    def joined(level):
        return lax.dot_general(
            mix_left[0, level],
            mix_right[0, level + 1],
            (((0,), (0,)), ((), ())),
            precision=lax.Precision.HIGHEST,
            preferred_element_type=jnp.float32,
        )

    lh, ll, rh, rl, mh, ml = split_into([core, 1 - core], 2, [weights, others])
    links = jnp.stack(after([lat_swap(joined(0), 2), lat_swap(joined(3), 16)], lh))
    kh, kl = split_into([core, 1 - core], 2, [[links], [core_swap(links)]])

    order = lax.dynamic_slice_in_dim(plan, core * own_cols, own_cols)
    chosen = (order[:, None] == jnp.arange(shots, dtype=plan.dtype)[None, :]).astype(jnp.float32)
    base = (lax.axis_index("lat") * row_count).astype(jnp.float32)
    shift = jnp.stack([base, jnp.zeros_like(base), base, jnp.zeros_like(base)])
    sources = (
        lax.dot_general(
            chosen,
            table,
            NT,
            precision=lax.Precision.HIGHEST,
            preferred_element_type=jnp.float32,
        )
        - shift[None, :]
    )

    wide, narrow = row_count, rank

    def outer_round(c, z, near, far):
        e = lat_swap(z, far)
        a = lat_swap(c, near)
        b = lat_swap(c, near | far)
        return e, a, b

    which = range(STREAMS)
    kept = jnp.zeros((ticks, 2, STREAMS, piece, row_count), jnp.float32)
    carried = [jnp.zeros((piece, row_count), jnp.float32) for _ in which]
    for tick in range(ticks):
        group = jnp.clip(tick - stage, 0, GROUPS - 1)
        parts = [
            lax.dynamic_slice_in_dim(sources, group * group_cols + s * piece, piece) for s in which
        ]
        state = [
            run(
                functools.partial(kernel_1, 0),
                [carried[s], parts[s], lh, ll, rh, rl],
                (wide, narrow, narrow),
            )
            for s in which
        ]
        for layer in range(2):
            got = [outer_round(state[s][1], state[s][2], 1, 2) for s in which]
            state = [
                run(
                    functools.partial(kernel_2, layer),
                    [state[s][0], got[s][1], got[s][2], got[s][0], kh, kl, mh, ml, rh, rl],
                    (wide, narrow),
                )
                for s in which
            ]
            mid = [lat_swap(state[s][1], 4) for s in which]
            state = [
                run(
                    functools.partial(kernel_3, layer),
                    [state[s][0], mid[s], mh, ml, rh, rl],
                    (wide, narrow, narrow),
                )
                for s in which
            ]
            got = [outer_round(state[s][1], state[s][2], 8, 16) for s in which]
            following = []
            for s in which:
                inputs = [state[s][0], got[s][1], got[s][2], got[s][0]]
                if layer == 0:
                    *rest, kept = run(
                        functools.partial(kernel_41, layer, (tick, layer, s)),
                        [*inputs, parts[s], kh, kl, mh, ml, lh, ll, rh, rl],
                        (wide, narrow, narrow),
                        kept,
                        [pltpu.VMEM((piece, row_count), jnp.float32), pltpu.SemaphoreType.DMA],
                    )
                    following.append(rest)
                else:
                    trace, kept = run(
                        functools.partial(kernel_4, layer, (tick, layer, s)),
                        [*inputs, kh, kl, mh, ml],
                        (wide,),
                        kept,
                        [pltpu.SemaphoreType.DMA],
                    )
                    if tick < ticks - 1:
                        following.append(next_stage(trace))
            state = following
        carried = state

    def taken(layer):
        zero = jnp.zeros_like(stage)
        rows = lax.dynamic_slice(
            kept, (stage, layer, zero, zero, zero), (GROUPS, 1, STREAMS, piece, row_count)
        )
        return rows.reshape(FRONTS // 2, front_cols, row_count)

    own, other = taken(core), core_swap(taken(1 - core))
    fronts = jnp.concatenate([jnp.where(core == 0, own, other), jnp.where(core == 0, other, own)])
    return fronts.transpose(0, 2, 1)[None]


def solution(mesh):
    return jax.shard_map(
        on_device,
        mesh=mesh,
        in_specs=(
            P("depth", "lat", None),
            P("depth", None, "lat", None),
            P("depth", None, "lat", None),
            P("depth", None),
            P("depth", None),
            P(),
        ),
        out_specs=P("depth", None, "lat", None),
        check_vma=False,
    )
```

```python
import functools
import math

import jax
import jax.numpy as jnp
from jax import lax
from jax.experimental import pallas as pl
from jax.experimental.pallas import tpu as pltpu
from jax.sharding import PartitionSpec as P


N = 16384
FRONTS = 6
STREAMS = 2
GROUPS = 2
HALVING = 1.0 / math.sqrt(2.0)
NT = (((1,), (1,)), ((), ()))
NN = (((1,), (0,)), ((), ()))


def lat_swap(x, bit):
    count = lax.axis_size("lat")
    return lax.ppermute(x, "lat", [(i, i ^ bit) for i in range(count)])


def core_swap(x):
    count = lax.axis_size("depth")
    return lax.ppermute(x, "depth", [(i, i ^ 1) for i in range(count)])


def next_stage(x):
    count = lax.axis_size("depth")
    return lax.ppermute(x, "depth", [(i, i + 2) for i in range(count - 2)])


def split(x):
    high = x.astype(jnp.bfloat16)
    low = (x - high.astype(jnp.float32)).astype(jnp.bfloat16)
    return high, low


def mm(x, w_high, w_low, dims):
    rows = x.shape[0]
    high, low = split(x)
    both = jnp.concatenate([high, low], axis=0)
    main = lax.dot_general(both, w_high, dims, preferred_element_type=jnp.float32)
    rest = lax.dot_general(high, w_low, dims, preferred_element_type=jnp.float32)
    return main[:rows] + (main[rows:] + rest)


def begin_layer(v, source_ref, layer, lh, ll, rh, rl, y_ref, c_ref, z_ref):
    cells = source_ref[:, 2 * layer : 2 * layer + 1]
    amps = source_ref[:, 2 * layer + 1 : 2 * layer + 2]
    rows = lax.broadcasted_iota(jnp.int32, v.shape, 1).astype(jnp.float32)
    v = v + jnp.where(rows == cells, amps, 0.0)
    y = mm(v, lh[layer, 0], ll[layer, 0], NT)
    y_ref[...] = y
    c_ref[...] = mm(y, rh[layer, 0], rl[layer, 0], NN)
    z_ref[...] = mm(y, rh[layer, 1], rl[layer, 1], NN)


def pair_step(y, a, b, e, layer, level, kh, kl, mh, ml):
    link = 0 if level == 0 else 1
    inner = HALVING * (e + mm(b, kh[layer, link], kl[layer, link], NN))
    y = HALVING * (y + mm(a, mh[layer, level], ml[layer, level], NT))
    return HALVING * (y + mm(inner, mh[layer, level + 1], ml[layer, level + 1], NT))


def kernel_1(layer, v, source, lh, ll, rh, rl, y_ref, c_ref, z_ref):
    begin_layer(v[...], source, layer, lh, ll, rh, rl, y_ref, c_ref, z_ref)


def kernel_2(layer, y, a, b, e, kh, kl, mh, ml, rh, rl, y_ref, c_ref):
    out = pair_step(y[...], a[...], b[...], e[...], layer, 0, kh, kl, mh, ml)
    y_ref[...] = out
    c_ref[...] = mm(out, rh[layer, 2], rl[layer, 2], NN)


def kernel_3(layer, y, a, mh, ml, rh, rl, y_ref, c_ref, z_ref):
    out = HALVING * (y[...] + mm(a[...], mh[layer, 2], ml[layer, 2], NT))
    y_ref[...] = out
    c_ref[...] = mm(out, rh[layer, 3], rl[layer, 3], NN)
    z_ref[...] = mm(out, rh[layer, 4], rl[layer, 4], NN)


def kernel_4(layer, place, y, a, b, e, kh, kl, mh, ml, kept_in, t_ref, kept, sem):
    t_ref[...] = pair_step(y[...], a[...], b[...], e[...], layer, 3, kh, kl, mh, ml)
    copy = pltpu.make_async_copy(t_ref, kept.at[place], sem)
    copy.start()
    copy.wait()


def kernel_41(layer, place, y, a, b, e, source, kh, kl, mh, ml, lh, ll, rh, rl, kept_in, y_ref, c_ref, z_ref, kept, t, sem):
    out = pair_step(y[...], a[...], b[...], e[...], layer, 3, kh, kl, mh, ml)
    t[...] = out
    copy = pltpu.make_async_copy(t, kept.at[place], sem)
    copy.start()
    begin_layer(out, source, layer + 1, lh, ll, rh, rl, y_ref, c_ref, z_ref)
    copy.wait()


def kernel_split(count, fills, slots, *refs):
    groups = [refs[count * n : count * (n + 1)] for n in range(fills)]
    outs = refs[-(3 * count + 1) : -(count + 1)]
    buffers, sems = refs[-(count + 1) : -1], refs[-1]
    queued = []
    for n, sources in enumerate(groups):
        for m in range(count):
            for level in range(buffers[m].shape[1]):
                copy = pltpu.make_async_copy(sources[m].at[level], buffers[m].at[n, level], sems.at[len(queued)])
                copy.start()
                queued.append((n, m, level, copy))
    for n, m, level, copy in queued:
        copy.wait()
        high, low = split(buffers[m][n, level])
        outs[2 * m][slots[n], level] = high
        outs[2 * m + 1][slots[n], level] = low


def kernel_after(*refs):
    del refs


IN_VMEM = pl.BlockSpec(memory_space=pltpu.VMEM)
IN_SMEM = pl.BlockSpec(memory_space=pltpu.SMEM)
IN_HBM = pl.BlockSpec(memory_space=pl.ANY)
PARAMS = pltpu.CompilerParams(vmem_limit_bytes=6 << 20)


def held(x):
    return pltpu.with_memory_space_constraint(x, pltpu.VMEM) if x.dtype == jnp.bfloat16 else x


def run(kernel, arrays, widths, kept=None, scratch=()):
    rows = arrays[0].shape[0]
    shapes = [jax.ShapeDtypeStruct((rows, width), jnp.float32) for width in widths]
    in_specs = [IN_VMEM] * len(arrays)
    out_specs = [IN_VMEM] * len(widths)
    operands = [held(x) for x in arrays]
    aliases = {}
    if kept is not None:
        aliases = {len(operands): len(shapes)}
        operands.append(pltpu.with_memory_space_constraint(kept, pltpu.HBM))
        in_specs.append(IN_HBM)
        out_specs.append(IN_HBM)
        shapes.append(jax.ShapeDtypeStruct(kept.shape, kept.dtype))
    return pl.pallas_call(
        kernel,
        out_shape=shapes,
        in_specs=in_specs,
        out_specs=out_specs,
        scratch_shapes=scratch,
        input_output_aliases=aliases,
        compiler_params=PARAMS,
    )(*operands)


def split_into(slots, total, groups, filled=None):
    count = len(groups[0])
    shapes = [
        pltpu.VMEM((total, *x.shape), jnp.bfloat16) for x in groups[0] for _ in range(2)
    ]
    sources = [pltpu.with_memory_space_constraint(x, pltpu.HBM) for group in groups for x in group]
    earlier = [held(x) for x in filled or []]
    chunks = sum(x.shape[0] for x in groups[0])
    return pl.pallas_call(
        functools.partial(kernel_split, count, len(groups)),
        out_shape=shapes,
        in_specs=[IN_SMEM] + [IN_HBM] * len(sources) + [IN_VMEM] * len(earlier),
        out_specs=[IN_VMEM] * len(shapes),
        scratch_shapes=[pltpu.VMEM((len(groups), *x.shape), jnp.float32) for x in groups[0]]
        + [pltpu.SemaphoreType.DMA((len(groups) * chunks,))],
        input_output_aliases={1 + len(sources) + n: n for n in range(len(earlier))},
        compiler_params=pltpu.CompilerParams(vmem_limit_bytes=16 << 20),
    )(jnp.stack(slots), *sources, *earlier)


def after(arrays, value):
    operands = [pltpu.with_memory_space_constraint(x, pltpu.HBM) for x in arrays]
    return pl.pallas_call(
        kernel_after,
        out_shape=[jax.ShapeDtypeStruct(x.shape, x.dtype) for x in arrays],
        in_specs=[IN_HBM] * (len(arrays) + 1),
        out_specs=[IN_HBM] * len(arrays),
        input_output_aliases={n: n for n in range(len(arrays))},
        compiler_params=pltpu.CompilerParams(vmem_limit_bytes=1 << 20),
    )(*operands, value)


def on_device(leaf_blocks, mix_left, mix_right, source_cells, source_amps, plan):
    depth_index = lax.axis_index("depth")
    core = lax.rem(depth_index, 2)
    stage = depth_index // 2
    stages = lax.axis_size("depth") // 2
    row_count = leaf_blocks.shape[1]
    rank = mix_left.shape[3]
    shots = plan.shape[0]
    front_cols = shots // FRONTS
    own_cols = shots // 2
    group_cols = own_cols // GROUPS
    piece = group_cols // STREAMS
    ticks = GROUPS + stages - 1

    table = jnp.concatenate([source_cells.astype(jnp.float32), source_amps * math.sqrt(N)], axis=0)
    swapped = core_swap(table)
    table = jnp.concatenate(
        [jnp.where(core == 0, table, swapped), jnp.where(core == 0, swapped, table)], axis=0
    )
    weights = [leaf_blocks, mix_right[0], mix_left[0]]
    others = [core_swap(x) for x in weights]

    def joined(level):
        return lax.dot_general(
            mix_left[0, level],
            mix_right[0, level + 1],
            (((0,), (0,)), ((), ())),
            precision=lax.Precision.HIGHEST,
            preferred_element_type=jnp.float32,
        )

    lh, ll, rh, rl, mh, ml = split_into([core, 1 - core], 2, [weights, others])
    links = jnp.stack(after([lat_swap(joined(0), 2), lat_swap(joined(3), 16)], lh))
    kh, kl = split_into([core, 1 - core], 2, [[links], [core_swap(links)]])

    order = lax.dynamic_slice_in_dim(plan, core * own_cols, own_cols)
    chosen = (order[:, None] == jnp.arange(shots, dtype=plan.dtype)[None, :]).astype(jnp.float32)
    base = (lax.axis_index("lat") * row_count).astype(jnp.float32)
    shift = jnp.stack([base, jnp.zeros_like(base), base, jnp.zeros_like(base)])
    sources = (
        lax.dot_general(
            chosen,
            table,
            NT,
            precision=lax.Precision.HIGHEST,
            preferred_element_type=jnp.float32,
        )
        - shift[None, :]
    )

    wide, narrow = row_count, rank

    def outer_round(c, z, near, far):
        e = lat_swap(z, far)
        a = lat_swap(c, near)
        b = lat_swap(c, near | far)
        return e, a, b

    which = range(STREAMS)
    kept = jnp.zeros((ticks, 2, STREAMS, piece, row_count), jnp.float32)
    carried = [jnp.zeros((piece, row_count), jnp.float32) for _ in which]
    for tick in range(ticks):
        group = jnp.clip(tick - stage, 0, GROUPS - 1)
        parts = [
            lax.dynamic_slice_in_dim(sources, group * group_cols + s * piece, piece) for s in which
        ]
        state = [
            run(
                functools.partial(kernel_1, 0),
                [carried[s], parts[s], lh, ll, rh, rl],
                (wide, narrow, narrow),
            )
            for s in which
        ]
        for layer in range(2):
            got = [outer_round(state[s][1], state[s][2], 1, 2) for s in which]
            state = [
                run(
                    functools.partial(kernel_2, layer),
                    [state[s][0], got[s][1], got[s][2], got[s][0], kh, kl, mh, ml, rh, rl],
                    (wide, narrow),
                )
                for s in which
            ]
            mid = [lat_swap(state[s][1], 4) for s in which]
            state = [
                run(
                    functools.partial(kernel_3, layer),
                    [state[s][0], mid[s], mh, ml, rh, rl],
                    (wide, narrow, narrow),
                )
                for s in which
            ]
            got = [outer_round(state[s][1], state[s][2], 8, 16) for s in which]
            following = []
            for s in which:
                inputs = [state[s][0], got[s][1], got[s][2], got[s][0]]
                if layer == 0:
                    *rest, kept = run(
                        functools.partial(kernel_41, layer, (tick, layer, s)),
                        [*inputs, parts[s], kh, kl, mh, ml, lh, ll, rh, rl],
                        (wide, narrow, narrow),
                        kept,
                        [pltpu.VMEM((piece, row_count), jnp.float32), pltpu.SemaphoreType.DMA],
                    )
                    following.append(rest)
                else:
                    trace, kept = run(
                        functools.partial(kernel_4, layer, (tick, layer, s)),
                        [*inputs, kh, kl, mh, ml],
                        (wide,),
                        kept,
                        [pltpu.SemaphoreType.DMA],
                    )
                    if tick < ticks - 1:
                        following.append(next_stage(trace))
            state = following
        carried = state

    def taken(layer):
        zero = jnp.zeros_like(stage)
        rows = lax.dynamic_slice(
            kept, (stage, layer, zero, zero, zero), (GROUPS, 1, STREAMS, piece, row_count)
        )
        return rows.reshape(FRONTS // 2, front_cols, row_count)

    own, other = taken(core), core_swap(taken(1 - core))
    fronts = jnp.concatenate([jnp.where(core == 0, own, other), jnp.where(core == 0, other, own)])
    return fronts.transpose(0, 2, 1)[None]


def solution(mesh):
    return jax.shard_map(
        on_device,
        mesh=mesh,
        in_specs=(
            P("depth", "lat", None),
            P("depth", None, "lat", None),
            P("depth", None, "lat", None),
            P("depth", None),
            P("depth", None),
            P(),
        ),
        out_specs=P("depth", None, "lat", None),
        check_vma=False,
    )
```
